32 devices in a mesh: rows: 4 (over y, x), cols: 8 (over z, core).
Axes of the slice: x: 2, y: 2, z: 4, core: 2. Of those that a mesh axis runs over, the one named last changes fastest.
Arguments:
- right_side: float32 [8192, 2048], P('rows', 'cols'), may hold values from -6 to 6
- inverse_blocks: float32 [8, 1024, 1024], P('rows', 'cols'), may hold values from -2 to 2, as said below
- coupling_blocks: float32 [8, 1024, 1024], P('rows', 'cols'), may hold values from -0.109375 to 0.109375
- prior_solution: float32 [1024, 2048], P(None, 'cols'), may hold values from -6 to 6
Outputs:
- solution: float32 [8192, 2048], P('rows', 'cols')
The draws below stay inside these ranges and needn't reach their ends.
Inputs may be any that keep to these rules, and one draw needn't show every extreme that they name: inverse_blocks holds the inverses of well conditioned diagonal blocks of the factor.
All inputs are finite; a program needn't handle non-finite values.
Results may differ from the reference program's by a relative error of at most 0.00013.
Values sent between devices are 32-bit elements; how exact they have to be, the bound alone decides.
No kernel may reach another device: no remote copies, remote signals or barrier semaphores. Data moves between devices by JAX's collectives and lax.ppermute only.
A program may use at most 128 MiB of HBM per device.

```python
import math
import jax
import jax.numpy as jnp
from jax import lax

BS = 1024
NB = 8
N = 8192
M = 2048


def draw_inverse_blocks(key, part):
    diag_key, off_key = jax.random.split(jax.random.fold_in(key, 11))
    diagonal = jax.random.uniform(diag_key, (NB, BS), jnp.float32, 0.8, 1.2)
    off_part = jnp.clip(jax.random.normal(off_key, (NB, BS, BS), jnp.float32), -6.0, 6.0) * (0.5 / math.sqrt(BS))
    identity = jnp.eye(BS, dtype=jnp.float32)
    return off_part + identity[None, :, :] * diagonal[:, :, None]


def steps_of(own_key, shape, cuts, smallest, high):
    def one(dim, shards_of):
        draws = jax.random.uniform(jax.random.fold_in(jax.random.fold_in(own_key, 6), dim), (shards_of,), jnp.float32, smallest / len(cuts), high / len(cuts))
        return jnp.repeat(jnp.exp(draws), shape[dim] // shards_of).reshape((-1,) + (1,) * (len(shape) - dim - 1))

    level = one(*cuts[0])
    for cut in cuts[1:]:
        level = level * one(*cut)
    return level


def normal_values(key, extent, deviation, reach, shards=(), held_as=jnp.bfloat16):
    array = deviation * jax.random.normal(key, extent, jnp.float32)
    if shards:
        array = array * steps_of(key, extent, shards, -0.22, 0.18)
    return jnp.clip(array, -reach, reach).astype(held_as)


def setup_inputs(seed: int = 0) -> dict:
    streams_of = jax.random.split(jax.random.key(seed), 5)
    right_side = normal_values(streams_of[0], (N, M), 1.0, 6.0, ((0, 4), (1, 8)), jnp.float32)
    inverse_blocks = draw_inverse_blocks(jax.random.fold_in(streams_of[4], 71), 0)
    coupling_blocks = normal_values(streams_of[2], (NB, BS, BS), (3 * BS) ** -0.5, 0.109375, ((0, 4), (1, 8)), jnp.float32)
    prior_solution = normal_values(streams_of[3], (BS, M), 1.0, 6.0, ((1, 8),), jnp.float32)
    return dict(right_side=right_side, inverse_blocks=inverse_blocks, coupling_blocks=coupling_blocks, prior_solution=prior_solution)


HIGHEST_PRECISION = lax.Precision.HIGHEST


def reference(right_side, inverse_blocks, coupling_blocks, prior_solution):
    blocks = right_side.reshape(NB, BS, M)

    def advance(previous, inputs):
        inverse, coupling, local_rhs = inputs
        pushed = local_rhs - jnp.dot(coupling, previous, precision=HIGHEST_PRECISION, preferred_element_type=jnp.float32)
        current = jnp.dot(inverse, pushed, precision=HIGHEST_PRECISION, preferred_element_type=jnp.float32)
        return current, current

    final_block, solved = lax.scan(advance, prior_solution, (inverse_blocks, coupling_blocks, blocks))
    return solved.reshape(NB * BS, M)
```

```python
import functools
import jax
import jax.numpy as jnp
from jax import lax
from jax.experimental import pallas as pl
from jax.experimental.pallas import tpu as pltpu
from jax.sharding import PartitionSpec as P


F32 = jnp.float32
BF16 = jnp.bfloat16
CORES = 2
PIECES = 4
LAG = 2
ANY = pl.BlockSpec(memory_space=pl.ANY)
VMEM = pl.BlockSpec(memory_space=pltpu.VMEM)
SMEM = pl.BlockSpec(memory_space=pltpu.SMEM)


def split(x):
    high = x.astype(BF16)
    return high, (x - high.astype(F32)).astype(BF16)


def dot(a, b):
    return jnp.dot(a, b, preferred_element_type=F32)


def dot3(a, b_high, b_low):
    a_high, a_low = split(a)
    return dot(a_high, b_high) + (dot(a_low, b_high) + dot(a_high, b_low))


def place(meta_ref, shards, plane, target, sems):
    rows = target.shape[0] // (len(shards) - 2)

    def copy(i):
        source = shards[i] if plane is None else shards[i].at[plane]
        start = pl.multiple_of(meta_ref[i] * rows, rows)
        return pltpu.make_async_copy(source, target.at[pl.ds(start, rows)], sems.at[i])

    for i in range(len(shards)):
        pl.when(meta_ref[i] >= 0)(lambda i=i: copy(i).start())

    def wait():
        for i in range(len(shards)):
            pl.when(meta_ref[i] >= 0)(lambda i=i: copy(i).wait())

    return wait


def first_kernel(count, *refs):
    meta = refs[0]
    shards = refs[1:1 + count]
    rhs, w_high, w_low, d0, held_c, held_a, c_high, c_low, sems = refs[1 + count:]
    wait_c = place(meta, shards, 0, held_c, sems.at[0])
    wait_a = place(meta, shards, 1, held_a, sems.at[1])
    size = held_c.shape[0]
    c_high[:, size:], c_low[:, size:] = split(rhs[...])
    wait_c()
    tile = 256

    @pl.loop(0, size // tile)
    def _(i):
        at = pl.ds(pl.multiple_of(i * tile, tile), tile)
        c_high[at, :size], c_low[at, :size] = split(held_c[at, :])

    wait_a()

    @pl.loop(0, size // tile)
    def _(i):
        at = pl.ds(pl.multiple_of(i * tile, tile), tile)
        product = dot3(held_a[at, :], c_high[...], c_low[...])
        w_high[at, :], w_low[at, :] = split(product)
        d0[at, :] = product[:, size:]


def second_kernel(count, *refs):
    meta = refs[0]
    shards = refs[1:1 + count]
    rhs, w_high, w_low, q_high, q_low, held, sems = refs[1 + count:]
    wait = place(meta, shards, None, held, sems)
    size = held.shape[0]
    tile = 256
    wait()

    @pl.loop(0, size // tile)
    def _(i):
        at = pl.ds(pl.multiple_of(i * tile, tile), tile)
        product = dot3(held[at, :], w_high[...], w_low[...])
        q_high[at, :size], q_low[at, :size] = split(product[:, :size])
        q_high[at, size:], q_low[at, size:] = split(rhs[at, :] - product[:, size:])


def pack(top, bottom, piece):
    lane = lax.broadcasted_iota(jnp.int32, top.shape, 1)
    half = top.shape[1] // 2
    if piece % 2 == 0:
        return jnp.where(lane < half, top, pltpu.roll(bottom, half, 1))
    return jnp.where(lane < half, pltpu.roll(top, half, 1), bottom)


def unpack(even, odd):
    lane = lax.broadcasted_iota(jnp.int32, even.shape, 1)
    half = even.shape[1] // 2
    top = jnp.where(lane < half, even, pltpu.roll(odd, half, 1))
    bottom = jnp.where(lane < half, pltpu.roll(even, half, 1), odd)
    return top, bottom


def pack_pieces(value, pieces):
    half = value.shape[0] // 2
    for piece in range(pieces.shape[0]):
        columns = slice((piece // 2) * 128, (piece // 2) * 128 + 128)
        pieces[piece] = pack(value[:half, columns], value[half:, columns], piece)


def pack_kernel(value, pieces):
    pack_pieces(value, pieces)


def third_kernel(count, *refs):
    meta = refs[0]
    shards = refs[1:1 + count]
    q_high, q_low, g_high, g_low, f_pieces, held, f_full, sems = refs[1 + count:]
    wait = place(meta, shards, None, held, sems)
    size = held.shape[0]
    tile = 256
    wait()

    @pl.loop(0, size // tile)
    def _(i):
        at = pl.ds(pl.multiple_of(i * tile, tile), tile)
        product = dot3(held[at, :], q_high[...], q_low[...])
        g_high[at, :], g_low[at, :] = split(product[:, :size])
        f_full[at, :] = product[:, size:]

    pack_pieces(f_full, f_pieces)


def step_kernel(first, *refs):
    if first is None:
        came, g_high, g_low, f_piece, out = refs
        x = came[...]
    else:
        group, came, mine, g_high, g_low, f_piece, out = refs
        x = jnp.where(group[0] == 0, mine[...], came[...])
    x_high, x_low = split(x)
    both = jnp.concatenate([x_high, x_low], axis=1)
    half, width = x.shape
    lane = lax.broadcasted_iota(jnp.int32, (half, width), 1)
    left = lane < width // 2

    def rows(at):
        parts = []
        for columns in (slice(0, half), slice(half, 2 * half)):
            wide = dot(g_high[at, columns], both)
            parts.append(wide[:, :width] + (wide[:, width:] + dot(g_low[at, columns], x_high)))
        return parts

    upper0, upper1 = rows(slice(0, half))
    lower0, lower1 = rows(slice(half, 2 * half))
    top = upper0 + pltpu.roll(upper1, width // 2, 1)
    bottom = pltpu.roll(lower0, width // 2, 1) + lower1
    out[...] = f_piece[...] + jnp.where(left, top, bottom)


def last_kernel(waves, lag, *refs):
    group = refs[0]
    came = refs[1:1 + waves]
    went = refs[1 + waves:1 + 2 * waves]
    w_high, w_low, d0, prior, out, x_in, x_out, sems = refs[1 + 2 * waves:]
    pieces = x_in.shape[0]
    g = group[0]
    groups = (waves - pieces) // lag + 1

    def each(act):
        for k in range(groups):
            def run(k=k):
                for i in range(pieces):
                    source = prior.at[i] if k == 0 else came[k * lag + i]
                    act(pltpu.make_async_copy(source, x_in.at[i], sems.at[0, i]))
                    act(pltpu.make_async_copy(went[k * lag + i], x_out.at[i], sems.at[1, i]))
            pl.when(g == k)(run)

    each(lambda c: c.start())
    each(lambda c: c.wait())
    half = x_in.shape[1]
    size = 2 * half
    for tile in range(pieces // 2):
        at = slice(tile * 128, tile * 128 + 128)
        top, bottom = unpack(x_out[2 * tile], x_out[2 * tile + 1])
        out[size:size + half, at] = top
        out[size + half:, at] = bottom
    tops, bottoms = zip(*[unpack(x_in[2 * t], x_in[2 * t + 1]) for t in range(pieces // 2)])
    x = jnp.concatenate([jnp.concatenate(tops, 1), jnp.concatenate(bottoms, 1)], 0)
    x_high, x_low = split(x)
    for r in range(0, size, 256):
        p_high, p_low = w_high[r:r + 256, :size], w_low[r:r + 256, :size]
        product = dot(p_high, x_high) + (dot(p_low, x_high) + dot(p_high, x_low))
        out[r:r + 256, :] = d0[r:r + 256, :] - product


def cost(flops, moved):
    return pl.CostEstimate(flops=int(flops), bytes_accessed=int(moved), transcendentals=0)


def params(mib):
    return pltpu.CompilerParams(vmem_limit_bytes=mib << 20)


def spread(unit):
    chip = lax.axis_index("cols") // CORES
    chips = lax.axis_size("cols") // CORES

    def move(x, pairs):
        full = [(a * CORES + c, b * CORES + c) for a, b in pairs for c in range(CORES)]
        return lax.ppermute(x, "cols", full)

    def swap(x):
        return lax.ppermute(x, "cols", [(q, q ^ 1) for q in range(chips * CORES)])

    left1 = move(unit, [(b, b - 1) for b in range(1, chips)])
    right1 = move(unit, [(b - 1, b) for b in range(1, chips)])
    ends = move(jnp.where(chip < 2, left1, right1), [(1, 0), (2, 3)])
    middle = move(jnp.where(chip < 2, right1, left1), [(1, 2), (2, 1)])
    second = jnp.where(jnp.logical_or(chip == 0, chip == 3), ends, middle)
    third = move(second, [(1, 0), (2, 3)])
    mine = [unit, left1, right1, second, third]
    return mine + [swap(x) for x in mine]


def places():
    q = lax.axis_index("cols")
    chip, core = q // CORES, q % CORES
    chips = lax.axis_size("cols") // CORES
    at = [
        chip,
        jnp.where(chip < chips - 1, chip + 1, -1),
        jnp.where(chip > 0, chip - 1, -1),
        (chip + 2) % chips,
        jnp.where(chip == 0, 3, jnp.where(chip == 3, 0, -1)),
    ]
    table = [jnp.where(a < 0, -1, a * CORES + (core if e == 0 else 1 - core)) for e in range(2) for a in at]
    return jnp.stack(table).astype(jnp.int32)


def gathered(unit):
    return [lax.all_gather(unit, "cols", axis=unit.ndim - 2, tiled=True)]


def solve(right_side, shards1, shards2, shards3, meta, prior):
    size = prior.shape[0]
    width = prior.shape[1]
    wide = size + width
    group = lax.axis_index("rows").astype(jnp.int32)
    groups = lax.axis_size("rows")
    count = len(shards1)
    b0, b1 = right_side[:size], right_side[size:]
    flops = 6 * size * size * wide

    def shape(*s, dtype=F32):
        return jax.ShapeDtypeStruct(s, dtype)

    sem = pltpu.SemaphoreType.DMA
    w_high, w_low, d0 = pl.pallas_call(
        functools.partial(first_kernel, count),
        out_shape=(shape(size, wide, dtype=BF16), shape(size, wide, dtype=BF16), shape(size, width)),
        in_specs=[SMEM] + [ANY] * count + [VMEM],
        out_specs=(VMEM,) * 3,
        scratch_shapes=[pltpu.VMEM((size, size), F32)] * 2
        + [pltpu.VMEM((size, wide), BF16)] * 2 + [sem((2, count))],
        compiler_params=params(32), cost_estimate=cost(flops, 20 << 20), name="stage1",
    )(meta, *shards1, b0)
    q_high, q_low = pl.pallas_call(
        functools.partial(second_kernel, count),
        out_shape=(shape(size, wide, dtype=BF16),) * 2,
        in_specs=[SMEM] + [ANY] * count + [VMEM] * 3,
        out_specs=(VMEM,) * 2,
        scratch_shapes=[pltpu.VMEM((size, size), F32), sem((count,))],
        compiler_params=params(32), cost_estimate=cost(flops, 16 << 20), name="stage2",
    )(meta, *shards2, b1, w_high, w_low)
    half = size // 2
    g_high, g_low, f_pieces = pl.pallas_call(
        functools.partial(third_kernel, count),
        out_shape=(shape(size, size, dtype=BF16),) * 2 + (shape(PIECES, half, 128),),
        in_specs=[SMEM] + [ANY] * count + [VMEM] * 2,
        out_specs=(VMEM,) * 3,
        scratch_shapes=[pltpu.VMEM((size, size), F32), pltpu.VMEM((size, width), F32), sem((count,))],
        compiler_params=params(32), cost_estimate=cost(flops, 16 << 20), name="stage3",
    )(meta, *shards3, q_high, q_low)
    prior_pieces = pl.pallas_call(
        pack_kernel, out_shape=shape(PIECES, half, 128), in_specs=[VMEM], out_specs=VMEM,
        compiler_params=params(8), cost_estimate=cost(size * width, 2 << 20), name="pack",
    )(prior)

    waves = PIECES + LAG * (groups - 1)
    pairs = [(i, i + 1) for i in range(groups - 1)]
    blank = jnp.zeros((half, 128), F32)
    came, went = [], []
    for wave in range(waves):
        arrived = lax.ppermute(went[wave - LAG], "rows", pairs) if wave >= LAG else blank
        if wave < PIECES:
            operands = (group[None], arrived, prior_pieces[wave])
            specs = [SMEM, VMEM, VMEM]
            kernel = functools.partial(step_kernel, True)
        else:
            operands, specs = (arrived,), [VMEM]
            kernel = functools.partial(step_kernel, None)
        own = jnp.clip(wave - LAG * group, 0, PIECES - 1)
        f_piece = lax.dynamic_index_in_dim(f_pieces, own, 0, keepdims=False)
        came.append(arrived)
        went.append(pl.pallas_call(
            kernel, out_shape=shape(half, 128), in_specs=specs + [VMEM] * 3, out_specs=VMEM,
            compiler_params=params(12), cost_estimate=cost(6 * size * size * 128, 6 << 20), name="step",
        )(*operands, g_high, g_low, f_piece))
    return pl.pallas_call(
        functools.partial(last_kernel, waves, LAG),
        out_shape=shape(2 * size, width),
        in_specs=[SMEM] + [ANY] * (2 * waves) + [VMEM] * 3 + [ANY],
        out_specs=VMEM,
        scratch_shapes=[pltpu.VMEM((PIECES, half, 128), F32)] * 2 + [sem((2, PIECES))],
        compiler_params=params(20), cost_estimate=cost(6 * size * size * width, 12 << 20), name="finish",
    )(group[None], *came, *went, w_high, w_low, d0, prior_pieces)


def local(right_side, inverse_blocks, coupling_blocks, prior_solution):
    unit1 = jnp.stack([coupling_blocks[0], inverse_blocks[0]])
    unit2, unit3 = coupling_blocks[1], inverse_blocks[1]
    if lax.axis_size("cols") == 4 * CORES:
        shards = [spread(u) for u in (unit1, unit2, unit3)]
        meta = places()
    else:
        blocks = lax.axis_size("cols")
        rows = unit2.shape[0]
        shards = []
        for unit in (unit1, unit2, unit3):
            full = lax.all_gather(unit, "cols", axis=unit.ndim - 2, tiled=True)
            part = full.shape[-2] // 8
            shards.append([full[..., i * part:(i + 1) * part, :] for i in list(range(8)) + [0, 0]])
        meta = jnp.array(list(range(8)) + [-1, -1], jnp.int32)
    return solve(right_side, *shards, meta, prior_solution)


def solution(mesh):
    placed = (P("rows", "cols"), P("rows", "cols", None), P("rows", "cols", None), P(None, "cols"))
    return jax.shard_map(
        local, mesh=mesh, in_specs=placed, out_specs=P("rows", "cols"), check_vma=False
    )
```
